32 devices in a mesh: enc: 4 (over y, x), seq: 2 (over core), tp: 4 (over z).
Axes of the slice: x: 2, y: 2, z: 4, core: 2. Of those that a mesh axis runs over, the one named last changes fastest.
Arguments:
- visual_key_value: bfloat16 [4, 16, 256, 2048], P(None, 'seq', 'enc', 'tp'), may hold values from -4.5 to 4.5
- patch_blocks: int32 [4, 16], P('enc'), may hold values from 1 to 8
- queries: bfloat16 [4, 4, 32, 8192], P('enc', 'seq', None, 'tp'), may hold values from -113 to 113
- suffix_key_value: bfloat16 [4, 4, 32, 2048], P('enc', 'seq', None, 'tp'), may hold values from -6 to 6
- suffix_hidden_state: bfloat16 [4, 4, 32, 8192], P('enc', 'seq', None, 'tp'), may hold values from -6 to 6
- down_weight: bfloat16 [8192, 128], P('tp'), may hold values from -0.0625 to 0.0625
- up_weight: bfloat16 [128, 8192], P(None, 'tp'), may hold values from -1.5 to 1.5
- question_adapter: int32 [4, 4], P('enc', 'seq'), may hold values from 0 to 7
- suffix_token_length: int32 [4, 4], P('enc', 'seq'), may hold values from 1 to 32
Outputs:
- context: bfloat16 [4, 4, 32, 8192], P('enc', 'seq', None, 'tp')
The draws below stay inside these ranges and needn't reach their ends.
All inputs are finite; a program needn't handle non-finite values.
Results may differ from the reference program's by a relative error of at most 0.0087.
Values may be sent and summed in bfloat16 or wider, within the bound.
No kernel may reach another device: no remote copies, remote signals or barrier semaphores. Data moves between devices by JAX's collectives and lax.ppermute only.
A program may use at most 64 MiB of HBM per device.

```python
import math
import jax
import jax.numpy as jnp
from jax import lax

MODEL_WIDTH = 8192
QUERY_HEADS = 64
KV_HEADS = 8
HEAD_SIZE = 128
ADAPTER_RANK = 16
ADAPTER_COUNT = 8
PAGES = 16
PAGE_TOK = 256
QTOK = 32
DOCS = 4
QUESTIONS = 4
KVW = 2048


def base_keys(key):
    values = jax.random.normal(jax.random.fold_in(key, 11), (DOCS, PAGES, PAGE_TOK, KVW), jnp.float32)
    return jnp.clip(values, -4.5, 4.5)


def draw_visual_key_value(key, part):
    values = base_keys(key)
    return values.astype(jnp.bfloat16)


def draw_queries(key, part):
    values = jax.random.normal(jax.random.fold_in(key, 23), (DOCS, QUESTIONS, QTOK, QUERY_HEADS * HEAD_SIZE), jnp.float32)
    values = jnp.clip(values, -4.5, 4.5)
    return values.astype(jnp.bfloat16)


def place_ends(values, own_key, least, largest):
    longest = values.shape.index(max(values.shape))
    spots = []
    for shift in (0, 1):
        where = [jax.random.randint(jax.random.fold_in(own_key, axis), (), 0, length) for axis, length in enumerate(values.shape)]
        where[longest] = (where[longest] + shift) % values.shape[longest]
        spots.append(tuple(where))
    return values.at[spots[0]].set(least).at[spots[1]].set(largest)


def block_scale(own_key, extent, cuts, smallest, high):
    factor_of = 1.0
    for axis_at, parts in cuts:
        draws = jax.random.uniform(jax.random.fold_in(jax.random.fold_in(own_key, 6), axis_at), (parts,), jnp.float32, smallest / len(cuts), high / len(cuts))
        factor_of = factor_of * jnp.repeat(jnp.exp(draws), extent[axis_at] // parts).reshape((-1,) + (1,) * (len(extent) - 1 - axis_at))
    return factor_of


def noise(stream_key, extent, scale, limit, pieces=(), kind=jnp.bfloat16):
    drawn = jax.random.normal(stream_key, extent, jnp.float32) * scale
    if len(pieces) > 0:
        drawn = block_scale(stream_key, extent, pieces, -0.22, 0.18) * drawn
    return jnp.clip(drawn, min=-limit, max=limit).astype(kind)


def setup_inputs(seed: int = 0) -> dict:
    keys = jax.random.split(jax.random.key(seed), 10)
    visual_key_value = draw_visual_key_value(jax.random.fold_in(keys[9], 71), 0)
    patch_blocks = place_ends(jax.random.randint(keys[1], (DOCS, PAGES), 1, 9), jax.random.fold_in(keys[1], 1), 1, 8).astype(jnp.int32)
    queries = draw_queries(jax.random.fold_in(keys[9], 71), 0)
    suffix_key_value = noise(keys[3], (DOCS, QUESTIONS, QTOK, KVW), 1.4, 6.0, ((0, 4), (1, 2), (3, 4)))
    suffix_hidden_state = noise(keys[4], (DOCS, QUESTIONS, QTOK, MODEL_WIDTH), 1.0, 6.0, ((0, 4), (1, 2), (3, 4)))
    down_weight = noise(keys[5], (MODEL_WIDTH, ADAPTER_COUNT * ADAPTER_RANK), MODEL_WIDTH ** -0.5, 0.0625, ((0, 4),))
    up_weight = noise(keys[6], (ADAPTER_COUNT * ADAPTER_RANK, QUERY_HEADS * HEAD_SIZE), ADAPTER_RANK ** -0.5, 1.5, ((1, 4),))
    question_adapter = place_ends(jax.random.randint(keys[7], (DOCS, QUESTIONS), 0, ADAPTER_COUNT), jax.random.fold_in(keys[7], 1), 0, ADAPTER_COUNT - 1).astype(jnp.int32)
    suffix_token_length = place_ends(jax.random.randint(keys[8], (DOCS, QUESTIONS), 1, QTOK + 1), jax.random.fold_in(keys[8], 1), 1, QTOK).astype(jnp.int32)
    return dict(visual_key_value=visual_key_value, patch_blocks=patch_blocks, queries=queries, suffix_key_value=suffix_key_value, suffix_hidden_state=suffix_hidden_state, down_weight=down_weight, up_weight=up_weight, question_adapter=question_adapter, suffix_token_length=suffix_token_length)


NEG_BIG = -1e+30
ADAPTER_SCALE = 2.0

def reference(visual_key_value, patch_blocks, queries, suffix_key_value, suffix_hidden_state, down_weight, up_weight, question_adapter, suffix_token_length):
    head_group = QUERY_HEADS // KV_HEADS
    inverse = 1.0 / math.sqrt(HEAD_SIZE)
    row_totals = DOCS * QUESTIONS * QTOK
    asked_rows = QUESTIONS * QTOK
    key_count = PAGES * PAGE_TOK
    hidden_state_rows = suffix_hidden_state.reshape(row_totals, MODEL_WIDTH)
    reduced_features = jnp.dot(hidden_state_rows, down_weight, preferred_element_type=jnp.float32)
    owning_question = jnp.arange(ADAPTER_COUNT * ADAPTER_RANK, dtype=jnp.int32) // ADAPTER_RANK
    row_ids = jnp.broadcast_to(question_adapter[:, :, None], (DOCS, QUESTIONS, QTOK)).reshape(row_totals, 1)
    selected_adapter = jnp.where(owning_question[None, :] == row_ids, reduced_features, 0.0).astype(jnp.bfloat16)
    raised_features = jnp.dot(selected_adapter, up_weight, preferred_element_type=jnp.float32)
    query_matrix = (queries.reshape(row_totals, QUERY_HEADS * HEAD_SIZE).astype(jnp.float32) + ADAPTER_SCALE * raised_features).astype(jnp.bfloat16)
    query_matrix = query_matrix.reshape(DOCS, asked_rows, KV_HEADS, head_group, HEAD_SIZE)
    visual = visual_key_value.reshape(DOCS, key_count, KV_HEADS, 2, HEAD_SIZE)
    token_pos = jnp.arange(PAGE_TOK, dtype=jnp.int32)
    live_keys = (8 * token_pos[None, None, :] < patch_blocks[:, :, None] * PAGE_TOK).reshape(DOCS, key_count)
    suffix_pairs = suffix_key_value.reshape(DOCS, QUESTIONS, QTOK, KV_HEADS, 2, HEAD_SIZE)
    positions = jnp.arange(QTOK, dtype=jnp.int32)
    causal = positions[None, :] <= positions[:, None]
    within = positions[None, None, :] < suffix_token_length[:, :, None]
    own_valid = causal[None, None, :, :] & within[:, :, None, :]

    def per_doc(doc_inputs):
        query_doc, visual_doc, live_doc, pairs_doc, valid_doc = doc_inputs

        def per_head(head_inputs):
            query_head, visual_head, pairs_head = head_inputs
            query_float = query_head.astype(jnp.float32)
            visual_scores = jnp.einsum('ngd,ld->ngl', query_float, visual_head[:, 0, :].astype(jnp.float32)) * inverse
            visual_scores = jnp.where(live_doc[None, None, :], visual_scores, NEG_BIG)
            query_split = query_float.reshape(QUESTIONS, QTOK, head_group, HEAD_SIZE)
            suffix_scores = jnp.einsum('qigd,qjd->qigj', query_split, pairs_head[:, :, 0, :].astype(jnp.float32)) * inverse
            suffix_mask = valid_doc[:, :, None, :]
            suffix_scores = jnp.where(suffix_mask, suffix_scores, NEG_BIG)
            row_peak = jnp.maximum(visual_scores.max(axis=-1), suffix_scores.max(axis=-1).reshape(asked_rows, head_group))
            visual_weights = jnp.where(live_doc[None, None, :], jnp.exp(visual_scores - row_peak[:, :, None]), 0.0)
            peak_split = row_peak.reshape(QUESTIONS, QTOK, head_group)
            suffix_weights = jnp.where(suffix_mask, jnp.exp(suffix_scores - peak_split[:, :, :, None]), 0.0)
            denominator = visual_weights.sum(axis=-1) + suffix_weights.sum(axis=-1).reshape(asked_rows, head_group)
            visual_rounded = lax.optimization_barrier(visual_weights.astype(jnp.bfloat16)).astype(jnp.float32)
            suffix_rounded = lax.optimization_barrier(suffix_weights.astype(jnp.bfloat16)).astype(jnp.float32)
            numerators = jnp.einsum('ngl,ld->ngd', visual_rounded, visual_head[:, 1, :].astype(jnp.float32))
            numerators = numerators + jnp.einsum('qigj,qjd->qigd', suffix_rounded, pairs_head[:, :, 1, :].astype(jnp.float32)).reshape(asked_rows, head_group, HEAD_SIZE)
            return numerators / denominator[:, :, None]
        heads_out = lax.map(per_head, (jnp.moveaxis(query_doc, 1, 0), jnp.moveaxis(visual_doc, 1, 0), jnp.moveaxis(pairs_doc, 2, 0)))
        return jnp.moveaxis(heads_out, 0, 1)
    outputs = lax.map(per_doc, (query_matrix, visual, live_keys, suffix_pairs, own_valid))
    outputs = outputs.reshape(DOCS, QUESTIONS, QTOK, QUERY_HEADS * HEAD_SIZE)
    kept_rows = positions[None, None, :] < suffix_token_length[:, :, None]
    return jnp.where(kept_rows[:, :, :, None], outputs, 0.0).astype(jnp.bfloat16)
```

```python
import functools
import math

import jax
import jax.numpy as jnp
from jax import lax
from jax.experimental import pallas as pl
from jax.experimental.pallas import tpu as pltpu
from jax.sharding import PartitionSpec as P

HEAD_SIZE = 128
ADAPTER_RANK = 16
ADAPTER_SCALE = 2.0
PATCH_UNITS = 8
LANES = 128
NEG_BIG = -1e30
LOG2_SCALE = math.log2(math.e) / math.sqrt(HEAD_SIZE)


def round_up(n, m):
    return -(-n // m) * m


class Layout:
    def __init__(self, enc, seq, kv_heads):
        self.enc, self.seq = enc, seq
        self.groups = math.gcd(seq, kv_heads)
        self.halves = seq // self.groups
        slow = max(d for d in range(1, enc + 1) if enc % d == 0 and d * d <= enc)
        self.slow, self.fast = slow, enc // slow
        self.swaps = self.slow == self.fast
        self.rows, self.tiles = self.slow, self.fast

    def split(self, e, c):
        a, b = e // self.fast, e % self.fast
        if not self.swaps:
            return a, b
        odd = c % 2
        return a + odd * (b - a), b + odd * (a - b)

    def join(self, r, t, c):
        if not self.swaps:
            return r * self.fast + t
        odd = c % 2
        a, b = r + odd * (t - r), t + odd * (r - t)
        return a * self.fast + b

    def pairs(self, dr, dt, dh, dc):
        out = []
        for e in range(self.enc):
            for s in range(self.seq):
                h, c = s // self.groups, s % self.groups
                r, t = self.split(e, c)
                src_e = self.join((r + dr) % self.rows, (t + dt) % self.tiles, c)
                src_s = (h + dh) % self.halves * self.groups + (c + dc) % self.groups
                out.append((src_e * self.seq + src_s, e * self.seq + s))
        return out


def fetch(x, lay, dr=0, dt=0, dh=0, dc=0):
    return lax.ppermute(x, ("enc", "seq"), lay.pairs(dr, dt, dh, dc))


def give_back(x, lay, dr, dh, dc):
    return lax.ppermute(x, ("enc", "seq"), [(d, s) for s, d in lay.pairs(dr, 0, dh, dc)])


def matmul_t(a, b):
    return lax.dot_general(a, b, (((1,), (1,)), ((), ())), preferred_element_type=jnp.float32)


def query_kernel(dims, meta, adapters, units, *refs):
    asked, suffix_len, groups, width, mask_width, terms, pages = dims
    lowered = refs[:terms]
    up, queries, full = refs[terms : terms + 3]
    pieces = refs[terms + 3 :]
    total = lowered[0][...]
    for ref in lowered[1:]:
        total = total + ref[...]
    owner = lax.broadcasted_iota(jnp.int32, total.shape, 1) // ADAPTER_RANK
    question = lax.broadcasted_iota(jnp.int32, total.shape, 0) // suffix_len
    wanted = jnp.zeros_like(owner)
    for q in range(asked):
        wanted = jnp.where(question == q, adapters[q], wanted)
    picked = jnp.where(owner == wanted, total, 0.0).astype(jnp.bfloat16)
    raised = jnp.dot(picked, up[...], preferred_element_type=jnp.float32)
    full[...] = (queries[...].astype(jnp.float32) + ADAPTER_SCALE * raised).astype(jnp.bfloat16)
    rows = total.shape[0]
    lane = lax.broadcasted_iota(jnp.int32, (rows, mask_width), 1)
    page = lane // PATCH_UNITS
    unit = lane % PATCH_UNITS
    live_units = jnp.zeros_like(lane)
    for p in range(pages):
        live_units = jnp.where(page == p, units[p], live_units)
    bias = jnp.where(unit < live_units, 0.0, NEG_BIG).astype(jnp.bfloat16)
    for dc in range(groups):
        group = lax.rem(meta[0] + (groups - dc), groups)
        start = pl.multiple_of(group * width, LANES)
        pieces[dc][:, :width] = full[:, pl.ds(start, width)]
        pieces[dc][:, width:] = bias


def attend_kernel(dims, meta, *refs):
    blocks, block_rows, width, mask_width, n_pieces, tile, page_tokens, carried, final = dims
    q_refs = refs[:blocks]
    kv_refs = refs[blocks : blocks + n_pieces]
    at = blocks + n_pieces
    if carried:
        old_o, old_s = refs[at : at + 2]
        at += 2
    outs = refs[at:-2]
    keys_ref, values_ref = refs[-2:]
    pages = kv_refs[0].shape[1]
    kv_width = kv_refs[0].shape[3]
    piece_keys = pages * tile
    kv_heads = kv_width // (2 * HEAD_SIZE)
    heads = width // HEAD_SIZE
    per_kv = heads // kv_heads
    lane = lax.broadcasted_iota(jnp.int32, (block_rows, LANES), 1)
    row_id = lax.broadcasted_iota(jnp.int32, (piece_keys, mask_width), 0)
    lane_id = lax.broadcasted_iota(jnp.int32, (piece_keys, mask_width), 1)
    stats = [jnp.zeros((block_rows, LANES), jnp.float32) for _ in range(blocks)]
    values_ref[:, HEAD_SIZE:] = jnp.ones((n_pieces * piece_keys, LANES), jnp.bfloat16)
    for n in range(n_pieces):
        token = meta[2 + 2 * n] * tile + row_id % tile
        target = (meta[3 + 2 * n] + row_id // tile) * PATCH_UNITS
        target = target + token * PATCH_UNITS // page_tokens
        spot = pl.ds(n * piece_keys, piece_keys)
        keys_ref[spot, HEAD_SIZE:] = jnp.where(lane_id == target, 1.0, 0.0).astype(jnp.bfloat16)
    stack = max(d for d in range(1, per_kv + 1) if per_kv % d == 0 and d * blocks * block_rows <= 512)
    for kv in range(kv_heads):
        for n in range(n_pieces):
            spot = pl.ds(n * piece_keys, piece_keys)
            piece = kv_refs[n][0].reshape(piece_keys, kv_width)
            base = kv * 2 * HEAD_SIZE
            keys_ref[spot, :HEAD_SIZE] = piece[:, base : base + HEAD_SIZE]
            values_ref[spot, :HEAD_SIZE] = piece[:, base + HEAD_SIZE : base + 2 * HEAD_SIZE]
        for first in range(kv * per_kv, (kv + 1) * per_kv, stack):
            parts = []
            for g in range(first, first + stack):
                for b in range(blocks):
                    head = q_refs[b][:, g * HEAD_SIZE : (g + 1) * HEAD_SIZE]
                    parts.append(jnp.concatenate([head, q_refs[b][:, width:]], axis=1))
            rows = jnp.concatenate(parts, axis=0)
            scores = matmul_t(rows, keys_ref[...])
            peak = scores.max(axis=1, keepdims=True) * LOG2_SCALE
            weights = jnp.exp2(scores * LOG2_SCALE - peak).astype(jnp.bfloat16)
            sums = jnp.dot(weights, values_ref[...], preferred_element_type=jnp.float32)
            denom = sums[:, HEAD_SIZE:]
            mean = sums[:, :HEAD_SIZE] / denom
            level = peak + jnp.log2(denom)
            i = 0
            for g in range(first, first + stack):
                cols = slice(g * HEAD_SIZE, (g + 1) * HEAD_SIZE)
                for b in range(blocks):
                    o = mean[i * block_rows : (i + 1) * block_rows]
                    s = level[i * block_rows : (i + 1) * block_rows]
                    i += 1
                    if carried:
                        s_old = jnp.broadcast_to(old_s[b, :, g : g + 1], s.shape)
                        top = jnp.maximum(s, s_old)
                        w_new, w_old = jnp.exp2(s - top), jnp.exp2(s_old - top)
                        both = w_new + w_old
                        o = (o * w_new + old_o[b, :, cols] * w_old) / both
                        s = top + jnp.log2(both)
                    if final:
                        outs[b][:, cols] = o.astype(jnp.bfloat16)
                        high = s.astype(jnp.bfloat16).astype(jnp.float32)
                        middle = (s - high).astype(jnp.bfloat16).astype(jnp.float32)
                        low = s - high - middle
                        keep = stats[b]
                        keep = jnp.where(lane == g, high, keep)
                        keep = jnp.where(lane == heads + g, middle, keep)
                        stats[b] = jnp.where(lane == 2 * heads + g, low, keep)
                    else:
                        outs[0][b, :, cols] = o
                        stats[b] = jnp.where(lane == g, s, stats[b])
    for b in range(blocks):
        if final:
            outs[b][:, width:] = stats[b].astype(jnp.bfloat16)
        else:
            outs[1][b] = stats[b]


def attend(q_blocks, pieces, carry, meta, page_tokens, final):
    blocks = len(q_blocks)
    block_rows = q_blocks[0].shape[0]
    pages, tile, kv_width = pieces[0][0].shape[1:3] + (pieces[0][2],)
    width = q_blocks[0].shape[1]
    mask_width = round_up(pieces[0][3] * PATCH_UNITS, LANES)
    width -= mask_width
    n_keys = len(pieces) * pages * tile
    dims = (blocks, block_rows, width, mask_width, len(pieces), tile, page_tokens, carry is not None, final)
    whole = lambda shape: pl.BlockSpec(shape, lambda i, m: (0,) * len(shape))
    in_specs = [whole(q.shape) for q in q_blocks]
    in_specs += [pl.BlockSpec((1, pages, tile, kv_width), p[1]) for p in pieces]
    operands = list(q_blocks) + [p[0] for p in pieces]
    if carry is not None:
        in_specs += [whole(x.shape) for x in carry]
        operands += list(carry)
    if final:
        out_shape = [jax.ShapeDtypeStruct((block_rows, width + LANES), jnp.bfloat16)] * blocks
    else:
        out_shape = [
            jax.ShapeDtypeStruct((blocks, block_rows, width), jnp.float32),
            jax.ShapeDtypeStruct((blocks, block_rows, LANES), jnp.float32),
        ]
    rows = blocks * block_rows * width // HEAD_SIZE
    return pl.pallas_call(
        functools.partial(attend_kernel, dims),
        out_shape=out_shape,
        grid_spec=pltpu.PrefetchScalarGridSpec(
            num_scalar_prefetch=1,
            grid=(1,),
            in_specs=in_specs,
            out_specs=[whole(s.shape) for s in out_shape],
            scratch_shapes=[
                pltpu.VMEM((n_keys, HEAD_SIZE + mask_width), jnp.bfloat16),
                pltpu.VMEM((n_keys, HEAD_SIZE + LANES), jnp.bfloat16),
            ],
        ),
        cost_estimate=pl.CostEstimate(
            flops=8 * rows * n_keys * HEAD_SIZE,
            bytes_accessed=n_keys * kv_width * 2,
            transcendentals=rows * n_keys,
        ),
        name="attend_final" if final else "attend_part",
    )(meta, *operands)


def suffix_kernel(dims, lengths, q_ref, kv_ref, o_ref, s_ref):
    asked, suffix_len, kv_heads, per_kv, groups = dims
    rows = asked * suffix_len
    shape = (per_kv * rows, rows)
    row = lax.broadcasted_iota(jnp.int32, shape, 0) % rows
    key = lax.broadcasted_iota(jnp.int32, shape, 1)
    question = key // suffix_len
    length = jnp.zeros_like(key)
    for q in range(asked):
        length = jnp.where(question == q, lengths[q], length)
    position = key % suffix_len
    seen = (row // suffix_len == question) & (position <= row % suffix_len) & (position < length)
    lane = lax.broadcasted_iota(jnp.int32, (rows, LANES), 1)
    heads = kv_heads * per_kv // groups
    for group in range(groups):
        stats = jnp.zeros((rows, LANES), jnp.float32)
        for kv in range(group * kv_heads // groups, (group + 1) * kv_heads // groups):
            base = kv * 2 * HEAD_SIZE
            first = kv * per_kv
            stacked = jnp.concatenate(
                [q_ref[:, g * HEAD_SIZE : (g + 1) * HEAD_SIZE] for g in range(first, first + per_kv)],
                axis=0,
            )
            scores = matmul_t(stacked, kv_ref[:, base : base + HEAD_SIZE])
            scores = jnp.where(seen, scores, NEG_BIG)
            peak = scores.max(axis=1, keepdims=True) * LOG2_SCALE
            weights = jnp.where(seen, jnp.exp2(scores * LOG2_SCALE - peak), 0.0)
            denom = weights.sum(axis=1, keepdims=True)
            sums = jnp.dot(
                weights.astype(jnp.bfloat16),
                kv_ref[:, base + HEAD_SIZE : base + 2 * HEAD_SIZE],
                preferred_element_type=jnp.float32,
            )
            live = denom > 0.0
            mean = sums / jnp.where(live, denom, 1.0)
            level = jnp.where(live, peak + jnp.log2(jnp.where(live, denom, 1.0)), NEG_BIG)
            for n in range(per_kv):
                g = first + n
                part = slice(n * rows, (n + 1) * rows)
                o_ref[:, g * HEAD_SIZE : (g + 1) * HEAD_SIZE] = mean[part]
                stats = jnp.where(lane == g - group * heads, level[part], stats)
        s_ref[group] = stats


def merge_kernel(dims, meta, lengths, *refs):
    asked, suffix_len, groups, width, per_group = dims
    parts = refs[: groups * per_group]
    own_o, own_s, out = refs[groups * per_group :]
    rows = asked * suffix_len
    heads = width // HEAD_SIZE
    row = lax.broadcasted_iota(jnp.int32, (rows, HEAD_SIZE), 0)
    length = jnp.zeros_like(row)
    for q in range(asked):
        length = jnp.where(row // suffix_len == q, lengths[q], length)
    kept = row % suffix_len < length
    for dc in range(groups):
        group = lax.rem(meta[0] + (groups - dc), groups)
        start = pl.multiple_of(group * width, LANES)
        mine = parts[dc * per_group : (dc + 1) * per_group]
        levels = [own_s[group]]
        for ref in mine:
            raw = ref[:, width:].astype(jnp.float32)
            levels.append(
                raw + pltpu.roll(raw, LANES - heads, 1) + pltpu.roll(raw, LANES - 2 * heads, 1)
            )
        top = functools.reduce(jnp.maximum, levels)
        shares = [jnp.exp2(x - top) for x in levels]
        scale = 1.0 / functools.reduce(jnp.add, shares)
        shares = [x * scale for x in shares]
        for g in range(heads):
            cols = slice(g * HEAD_SIZE, (g + 1) * HEAD_SIZE)
            spot = pl.ds(pl.multiple_of(start + g * HEAD_SIZE, LANES), HEAD_SIZE)
            total = own_o[:, spot] * shares[0][:, g : g + 1]
            for ref, share in zip(mine, shares[1:]):
                total = total + ref[:, cols].astype(jnp.float32) * share[:, g : g + 1]
            out[:, spot] = jnp.where(kept, total, 0.0).astype(jnp.bfloat16)


def per_device(
    visual_key_value,
    patch_blocks,
    queries,
    suffix_key_value,
    suffix_hidden_state,
    down_weight,
    up_weight,
    question_adapter,
    suffix_token_length,
):
    docs_here, asked, suffix_len, query_width = queries.shape
    kv_local = suffix_key_value.shape[3] // (2 * HEAD_SIZE)
    enc, seq, tp = lax.axis_size("enc"), lax.axis_size("seq"), lax.axis_size("tp")
    lay = Layout(enc, seq, kv_local)
    groups, halves = lay.groups, lay.halves
    page_local, tile = visual_key_value.shape[1:3]
    pages = page_local * seq
    page_tokens = tile * enc
    rows = asked * suffix_len
    width = query_width // groups
    kv_width = visual_key_value.shape[3] // groups
    mask_width = round_up(pages * PATCH_UNITS, LANES)
    e, s = lax.axis_index("enc"), lax.axis_index("seq")
    h, c = s // groups, s % groups
    r, t = lay.split(e, c)
    core = c.reshape(1).astype(jnp.int32)
    vmem = pl.BlockSpec(memory_space=pltpu.VMEM)
    smem = pl.BlockSpec(memory_space=pltpu.SMEM)
    results = []
    for here in range(docs_here):

        def tile_slice(dt, dc, dr):
            to_core = (c + groups - dc) % groups
            r_to, t_to = lay.split(e, to_core)
            t_to = (t_to + lay.tiles - dt) % lay.tiles
            doc = lay.join((r_to + dr) % lay.rows, t_to, to_core) * docs_here + here
            return lax.dynamic_slice(
                visual_key_value,
                (doc, 0, 0, to_core * kv_width),
                (1, page_local, tile, kv_width),
            )

        order = [*range(1, lay.rows), 0]
        near = [dc for dc in range(1, groups)]
        far = [(dt, dc) for dt in range(1, lay.tiles) for dc in range(groups)]
        arrived = {}
        for dr in order[:-1]:
            for dt, dc in far:
                arrived[dr, dt, dc] = (fetch(tile_slice(dt, dc, dr), lay, 0, dt, 0, dc), 0)

        hidden = suffix_hidden_state[here].reshape(rows, suffix_hidden_state.shape[3])
        lowered = jnp.dot(hidden, down_weight, preferred_element_type=jnp.float32)
        terms = [lowered]
        for d in range(1, tp):
            terms.append(lax.ppermute(lowered, "tp", [(i, (i + d) % tp) for i in range(tp)]))

        for dc in near:
            both = jnp.concatenate([tile_slice(0, dc, dr) for dr in range(lay.rows)], axis=0)
            moved = fetch(both, lay, 0, 0, 0, dc)
            for dr in range(lay.rows):
                arrived[dr, 0, dc] = (moved, dr)
        for dt, dc in far:
            arrived[0, dt, dc] = (fetch(tile_slice(dt, dc, 0), lay, 0, dt, 0, dc), 0)

        q_dims = (asked, suffix_len, groups, width, mask_width, tp, pages)
        q_full, *q_pieces = pl.pallas_call(
            functools.partial(query_kernel, q_dims),
            out_shape=[jax.ShapeDtypeStruct((rows, query_width), jnp.bfloat16)]
            + [jax.ShapeDtypeStruct((rows, width + mask_width), jnp.bfloat16)] * groups,
            in_specs=[smem] * 3 + [vmem] * (tp + 2),
            out_specs=[vmem] * (1 + groups),
            name="make_queries",
        )(
            core,
            question_adapter[here],
            patch_blocks[here],
            *terms,
            up_weight,
            queries[here].reshape(rows, query_width),
        )

        shifts = [(dh, dc) for dh in range(halves) for dc in range(groups)]
        q_blocks = {}
        for dr in [*order[:-1], 0]:
            for dh, dc in shifts:
                piece = q_pieces[dc]
                q_blocks[dr, dh, dc] = piece if dr == dh == dc == 0 else fetch(piece, lay, dr, 0, dh, dc)

        own_o, own_s = pl.pallas_call(
            functools.partial(
                suffix_kernel,
                (asked, suffix_len, kv_local, query_width // (kv_local * HEAD_SIZE), groups),
            ),
            out_shape=[
                jax.ShapeDtypeStruct((rows, query_width), jnp.float32),
                jax.ShapeDtypeStruct((groups, rows, LANES), jnp.float32),
            ],
            in_specs=[smem] + [vmem] * 2,
            out_specs=[vmem] * 2,
            name="attend_suffix",
        )(
            suffix_token_length[here],
            q_full,
            suffix_key_value[here].reshape(rows, suffix_key_value.shape[3]),
        )

        def pieces_of(dr, spots):
            doc = lay.join((r + dr) % lay.rows, t, c) * docs_here + here
            meta = [c, doc]
            out = []
            for dt, dc in spots:
                meta += [
                    lay.join(r, (t + dt) % lay.tiles, c),
                    (h * groups + (c + dc) % groups) * page_local,
                ]
                if dt == dc == 0:
                    out.append((visual_key_value, lambda i, m: (m[1], 0, 0, m[0]), kv_width, pages))
                else:
                    array, at = arrived[dr, dt, dc]
                    out.append((array, lambda i, m, at=at: (at, 0, 0, 0), kv_width, pages))
            return out, jnp.stack(meta).astype(jnp.int32)

        home = [(0, dc) for dc in range(groups)]
        done = {}
        for dr in order:
            blocks = [q_blocks[dr, dh, dc] for dh, dc in shifts]
            carry = None
            spots = home + far
            if dr == 0 and far:
                found, meta = pieces_of(dr, home)
                carry = attend(blocks, found, None, meta, page_tokens, False)
                spots = far
            found, meta = pieces_of(dr, spots)
            outs = attend(blocks, found, carry, meta, page_tokens, True)
            for (dh, dc), out in zip(shifts, outs):
                done[dr, dh, dc] = out if dr == dh == dc == 0 else give_back(out, lay, dr, dh, dc)

        parts = [
            done[dr, dh, dc] for dc in range(groups) for dr in range(lay.rows) for dh in range(halves)
        ]
        out = pl.pallas_call(
            functools.partial(merge_kernel, (asked, suffix_len, groups, width, lay.rows * halves)),
            out_shape=jax.ShapeDtypeStruct((rows, query_width), jnp.bfloat16),
            in_specs=[smem] * 2 + [vmem] * (len(parts) + 2),
            out_specs=vmem,
            name="merge",
        )(core, suffix_token_length[here], *parts, own_o, own_s)
        results.append(out.reshape(asked, suffix_len, query_width))
    return jnp.stack(results)


def solution(mesh):
    placed = (
        P(None, "seq", "enc", "tp"),
        P("enc", None),
        P("enc", "seq", None, "tp"),
        P("enc", "seq", None, "tp"),
        P("enc", "seq", None, "tp"),
        P("tp", None),
        P(None, "tp"),
        P("enc", "seq"),
        P("enc", "seq"),
    )
    return jax.shard_map(
        per_device,
        mesh=mesh,
        in_specs=placed,
        out_specs=P("enc", "seq", None, "tp"),
        check_vma=False,
    )
```
